32 devices in a mesh: dp: 1, expert: 32 (over z, y, x, core).
Axes of the slice: x: 2, y: 2, z: 4, core: 2. Of those that a mesh axis runs over, the one named last changes fastest.
Arguments:
- out_grad: bfloat16 [4096, 3584], P(('dp', 'expert')), may hold values from -6 to 6
- inputs: bfloat16 [4096, 3584], P(('dp', 'expert')), may hold values from -6 to 6
- router_weight: float32 [3584, 32], P('expert'), may hold values from -0.09375 to 0.09375
- routes: int32 [4096, 8], P(('dp', 'expert')), may hold values from 0 to 31, all different within a row; in each aligned block of 128 rows (0 to 127, 128 to 255, ...) at most 40 rows name the same one
- saved_hidden: bfloat16 [40960, 1024], P(('dp', 'expert')), may hold values from -0.5 to 0.5
- down_weight: bfloat16 [32, 1024, 3584], P('expert', None, 'dp'), may hold values from -0.1875 to 0.1875
Outputs:
- hidden_grad: bfloat16 [40960, 1024], P(('dp', 'expert'))
- input_grad: bfloat16 [4096, 3584], P(('dp', 'expert'))
- gate_grad: float32 [4096, 8], P(('dp', 'expert'))
- router_grad: float32 [3584, 32], P('expert')
The draws below stay inside these ranges and needn't reach their ends.
Inputs may be any that keep to these rules, and one draw needn't show every extreme that they name: `routes`: each row names 8 different experts. Within the rows of one device (aligned blocks of 128 rows) no expert is named by more than 40 rows, a bound that some block reaches.
All inputs are finite; a program needn't handle non-finite values.
Results may differ from the reference program's by a relative error of at most 0.0048.
Values may be sent and summed in bfloat16 or wider, within the bound.
A program may use at most 128 MiB of HBM per device.

```python
import math
import jax
import jax.numpy as jnp
import numpy as np
from jax import lax

D = 3584
FF = 1024
TOPK = 8
TOK_DEV = 128
EXPERTS = 32
CAP = 40
SLOTS = 1280
TOKENS = 4096
N_DP = 1


def steps_of(own_key, dims, pieces, smallest, top_value):
    gain = 1.0
    for dim, parts in pieces:
        heights = jax.random.uniform(jax.random.fold_in(jax.random.fold_in(own_key, 6), dim), (parts,), jnp.float32, smallest / len(pieces), top_value / len(pieces))
        gain = gain * jnp.repeat(jnp.exp(heights), dims[dim] // parts).reshape((-1,) + (1,) * (len(dims) - 1 - dim))
    return gain


def assign_block(own_key, own, number, rows, number_of, top, bound, slope):
    sequence = jax.random.permutation(own_key, number_of)
    crowded, usual = portions_of(number_of, rows * top, bound, slope, True), portions_of(number_of, rows * top, bound, slope, False)
    places = jnp.arange(number_of)

    def named(lengths, turn):
        used = int((lengths > 0).sum())
        fixed = max(1, used // 4)
        passed = fixed + (places - fixed + turn * (used - fixed)) % max(1, number_of - fixed)
        return jnp.zeros((number_of,), jnp.int32).at[sequence[jnp.where(places < fixed, places, passed)]].set(jnp.asarray(lengths, jnp.int32))

    lengths = jnp.where(number % 4 == 0, named(crowded, number // 4), named(usual, number - number // 4 - 1))
    mixed = jax.random.permutation(jax.random.fold_in(own, 3), number_of)
    source_of, receiver = mixed[0:number_of // 2 * 2:2], mixed[1:number_of // 2 * 2:2]
    room = jnp.minimum(lengths[source_of] - 1, bound - lengths[receiver]) // 2
    room = jnp.where((source_of == sequence[0]) | (receiver == sequence[0]) | (lengths[receiver] == 0), 0, jnp.maximum(room, 0))
    passed = jax.random.randint(jax.random.fold_in(own, 4), (number_of // 2,), 0, 1 << 20) % (room + 1)
    lengths = lengths.at[source_of].add(-passed).at[receiver].add(passed)
    members = jnp.searchsorted(jnp.cumsum(lengths), jnp.arange(rows * top), side="right").astype(jnp.int32)
    listing = members.reshape(top, rows).T
    listing = listing[jax.random.permutation(jax.random.fold_in(own, 1), rows)]
    turn = jax.random.randint(jax.random.fold_in(own, 2), (rows, 1), 0, top)
    return jnp.take_along_axis(listing, (jnp.arange(top)[None, :] + turn) % top, axis=1)


def portions_of(count, total, reach, slope, full):
    weights = [(1 << 20) // math.isqrt(rank ** slope) + 1 for rank in range(1, count + 1)]
    largest = reach if full else min(reach, max(-(-total // count), total * weights[0] // sum(weights)))
    least = 1 if total - largest >= count - 1 else 0
    holding, rest = [largest] + [least] * (count - 1), total - largest - least * (count - 1)
    while rest > 0:
        free = [i for i in range(1, count) if holding[i] < largest] or [i for i in range(1, count) if holding[i] < reach]
        mass, budget = sum([weights[i] for i in free]), rest
        for i in free:
            addition = min(reach - holding[i], max(1, budget * weights[i] // mass), rest)
            holding[i] = holding[i] + addition
            rest = rest - addition
    return np.array(holding)


def noise(key, dims, deviation, bound, pieces=(), kind=jnp.bfloat16):
    values = jax.random.normal(key, dims, jnp.float32) * deviation
    if len(pieces) > 0:
        values = steps_of(key, dims, pieces, -0.22, 0.18) * values
    return jnp.clip(values, min=-bound, max=bound).astype(kind)


def setup_inputs(seed: int = 0) -> dict:
    splits = jax.random.split(jax.random.key(seed), 7)
    out_grad = noise(splits[0], (TOKENS, D), 1.0, 6.0, ((0, 32),))
    inputs = noise(splits[1], (TOKENS, D), 1.0, 6.0, ((0, 32),))
    router_weight = noise(splits[2], (D, EXPERTS), D ** -0.5, 0.09375, ((0, 32),), jnp.float32)
    routes_keys = jax.random.split(jax.random.fold_in(splits[3], 1), TOKENS // TOK_DEV)
    routes_turns = jax.random.permutation(jax.random.fold_in(splits[3], 3), TOKENS // TOK_DEV)
    routes = jax.vmap(lambda own, number: assign_block(jax.random.fold_in(splits[3], 2), own, number, TOK_DEV, EXPERTS, TOPK, CAP, 2))(routes_keys, routes_turns).reshape((TOKENS, TOPK))
    saved_hidden = noise(splits[4], (N_DP * EXPERTS * SLOTS, FF), 0.0625, 0.5, ((0, 32),))
    down_weight = noise(splits[5], (EXPERTS, FF, D), FF ** -0.5, 0.1875, ((0, 32),))
    return dict(out_grad=out_grad, inputs=inputs, router_weight=router_weight, routes=routes, saved_hidden=saved_hidden, down_weight=down_weight)


ROUTE_SCALE = 2.5


def slot_numbers(routes):
    blocks = routes.reshape(-1, TOK_DEV * TOPK)
    expert_grid = jnp.arange(EXPERTS, dtype=jnp.int32)

    def one_block(expert_ids):
        onehot = (expert_ids[:, None] == expert_grid[None, :]).astype(jnp.int32)
        earlier = jnp.cumsum(onehot, axis=0) - onehot
        return jnp.sum(earlier * onehot, axis=1).astype(jnp.int32)

    position = lax.map(one_block, blocks)
    source = jnp.arange(blocks.shape[0], dtype=jnp.int32)
    group_id = source // EXPERTS
    local_id = source % EXPERTS
    slot_index = (group_id[:, None] * EXPERTS + blocks) * SLOTS + local_id[:, None] * CAP + position
    return slot_index.reshape(-1, TOPK).astype(jnp.int32)


def reference(out_grad, inputs, router_weight, routes, saved_hidden, down_weight):
    precise = lax.Precision.HIGHEST
    inputs_wide = inputs.astype(jnp.float32)
    logits = jnp.dot(inputs_wide, router_weight, precision=precise)
    scores = jax.nn.sigmoid(logits)
    chosen = jnp.take_along_axis(scores, routes, axis=1)
    totals = jnp.sum(chosen, axis=1, keepdims=True)
    gate_values = ROUTE_SCALE * chosen / totals
    sent_gate = lax.optimization_barrier(gate_values.astype(jnp.bfloat16)).astype(jnp.float32)
    slot_index = slot_numbers(routes)
    flat_slots = slot_index.reshape(-1)
    all_slots = N_DP * EXPERTS * SLOTS
    token_numbers = jnp.repeat(jnp.arange(TOKENS, dtype=jnp.int32), TOPK)
    slot_token = jnp.full((all_slots,), TOKENS, dtype=jnp.int32).at[flat_slots].set(token_numbers)
    slot_gate = jnp.zeros((all_slots,), jnp.float32).at[flat_slots].set(sent_gate.reshape(-1))
    padded_grad = jnp.concatenate([out_grad, jnp.zeros((1, D), jnp.bfloat16)], axis=0)
    copies = N_DP * EXPERTS

    def one_expert(packed):
        token_rows, gate_rows, hidden_rows, copy_id = packed
        weight = lax.dynamic_index_in_dim(down_weight, copy_id % EXPERTS, keepdims=False)
        gathered = padded_grad[token_rows]
        raw_grad = jnp.dot(gathered, weight.T, preferred_element_type=jnp.float32)
        hidden_part = (gate_rows[:, None] * raw_grad).astype(jnp.bfloat16)
        gate_part = jnp.sum(raw_grad * hidden_rows.astype(jnp.float32), axis=1)
        return hidden_part, gate_part

    hidden_grad, gate_terms = lax.map(one_expert, (slot_token.reshape(copies, SLOTS), slot_gate.reshape(copies, SLOTS), saved_hidden.reshape(copies, SLOTS, FF), jnp.arange(copies, dtype=jnp.int32)))
    hidden_grad = hidden_grad.reshape(all_slots, FF)
    gate_grad = gate_terms.reshape(-1)[slot_index]
    weighted = jnp.sum(gate_grad * gate_values, axis=1, keepdims=True)
    chosen_grad = (ROUTE_SCALE * gate_grad - weighted) / totals * chosen * (1.0 - chosen)
    token_index = jnp.arange(TOKENS, dtype=jnp.int32)[:, None]
    logit_grad = jnp.zeros((TOKENS, EXPERTS), jnp.float32).at[token_index, routes].add(chosen_grad)
    input_grad = jnp.dot(logit_grad, router_weight.T, precision=precise).astype(jnp.bfloat16)
    router_grad = jnp.dot(inputs_wide.T, logit_grad, precision=precise)
    return hidden_grad, input_grad, gate_grad, router_grad
```

```python
import jax
import jax.numpy as jnp
from jax import lax
from jax.experimental import pallas as pl
from jax.experimental.pallas import tpu as pltpu
from jax.sharding import PartitionSpec as P

ROUTE_SCALE = 2.5
MESH_ID = pl.DeviceIdType.MESH
UP, DOWN, XWAY, YWAY, PAIR, LOCAL = range(6)


def gather_kernel(rows_ref, weight_ref, rows_out, weight_out, send, recv, pair_recv, weight_send, weight_recv, own_sem):
    me = lax.axis_index("expert")
    core, x, y, z = me % 2, (me // 2) % 2, (me // 4) % 2, me // 8
    half = rows_ref.shape[0] // 2

    def number(xx, yy, zz, cc):
        return ((zz * 2 + yy) * 2 + xx) * 2 + cc

    barrier = pltpu.get_barrier_semaphore()

    def greet(i, carry):
        pl.semaphore_signal(barrier, inc=1, device_id={"expert": (me + i) % 32}, device_id_type=MESH_ID)
        return carry

    lax.fori_loop(1, 32, greet, 0)
    pl.semaphore_wait(barrier, 31)

    def weight_copy(to):
        return pltpu.make_async_remote_copy(
            src_ref=weight_ref, dst_ref=weight_out.at[me], send_sem=weight_send.at[to], recv_sem=weight_recv.at[me],
            device_id={"expert": to}, device_id_type=MESH_ID)

    def weight_arrival(source):
        return pltpu.make_async_remote_copy(
            src_ref=weight_ref, dst_ref=weight_out.at[source], send_sem=weight_send.at[source], recv_sem=weight_recv.at[source],
            device_id={"expert": source}, device_id_type=MESH_ID)

    def block(origin, part):
        return rows_out.at[origin, pl.ds(part * half, half)]

    def copy(origin, part, way, own=False):
        target = {
            UP: lambda: number(x, y, z + 1, core), DOWN: lambda: number(x, y, z - 1, core),
            XWAY: lambda: number(1 - x, y, z, core), YWAY: lambda: number(x, 1 - y, z, core),
            PAIR: lambda: number(x, y, z, 1 - core)}[way]()
        chip = origin // 2
        arrived = pair_recv if way == PAIR else recv
        return pltpu.make_async_remote_copy(
            src_ref=rows_ref.at[pl.ds(part * half, half)] if own else block(origin, part),
            dst_ref=block(origin, part), send_sem=send.at[way, chip, part], recv_sem=arrived.at[chip, part],
            device_id={"expert": target}, device_id_type=MESH_ID)

    def for_z(origin_step, act):
        if origin_step == 0:
            act()
        elif origin_step > 0:
            pl.when(z + origin_step <= 3)(act)
        else:
            pl.when(z + origin_step >= 0)(act)

    def along_z(step):
        own = step == 0

        def act():
            origin = number(x, y, z + step, core)
            for part in range(2):
                if not own:
                    copy(origin, part, XWAY).wait_recv()
                if step >= 0:
                    pl.when(z >= 1)(lambda: copy(origin, part, DOWN, own).start())
                if step <= 0:
                    pl.when(z <= 2)(lambda: copy(origin, part, UP, own).start())
                copy(origin, part, XWAY, own).start()
                copy(origin, part, YWAY, own).start()
                copy(origin, part, PAIR, own).start()

        for_z(step, act)

    def across(step):
        def act():
            from_x = number(1 - x, y, z + step, core)
            from_y = number(x, 1 - y, z + step, core)
            for part in range(2):
                copy(from_x, part, XWAY).wait_recv()
                if part == 0:
                    copy(from_x, part, YWAY).start()
                copy(from_x, part, PAIR).start()
                copy(from_y, part, YWAY).wait_recv()
                if part == 1:
                    copy(from_y, part, XWAY).start()
                copy(from_y, part, PAIR).start()

        for_z(step, act)

    def diagonal(step):
        def act():
            origin = number(1 - x, 1 - y, z + step, core)
            for part in range(2):
                copy(origin, part, XWAY).wait_recv()
                copy(origin, part, PAIR).start()

        for_z(step, act)

    def finish(step):
        def act():
            own = step == 0
            origin = number(x, y, z + step, core)
            for part in range(2):
                if step >= 0:
                    pl.when(z >= 1)(lambda: copy(origin, part, DOWN, own).wait_send())
                if step <= 0:
                    pl.when(z <= 2)(lambda: copy(origin, part, UP, own).wait_send())
                copy(origin, part, XWAY, own).wait_send()
                copy(origin, part, YWAY, own).wait_send()
            copy(number(1 - x, y, z + step, core), 0, YWAY).wait_send()
            copy(number(x, 1 - y, z + step, core), 1, XWAY).wait_send()

        for_z(step, act)

    own_copy = pltpu.make_async_copy(rows_ref, rows_out.at[me], own_sem.at[0])
    own_weight = pltpu.make_async_copy(weight_ref, weight_out.at[me], own_sem.at[1])

    def send_weight(i, carry):
        weight_copy((me + i) % 32).start()
        return carry

    lax.fori_loop(1, 32, send_weight, 0)
    along_z(0)
    own_copy.start()
    own_weight.start()
    for step in (1, -1):
        along_z(step)
    across(0)
    for step in (2, -2):
        along_z(step)
    for step in (1, -1):
        across(step)
    diagonal(0)
    for step in (3, -3):
        along_z(step)
    for step in (2, -2):
        across(step)
    for step in (1, -1):
        diagonal(step)
    for step in (3, -3):
        across(step)
    for step in (2, -2, 3, -3):
        diagonal(step)
    for step in (0, 1, -1, 2, -2, 3, -3):
        finish(step)
    own_copy.wait()
    own_weight.wait()

    def end_pair(i, carry):
        for part in range(2):
            copy(i * 2 + core, part, PAIR).wait_send()
            copy(i * 2 + 1 - core, part, PAIR).wait_recv()
        return carry

    lax.fori_loop(0, 16, end_pair, 0)

    def end_weight(i, carry):
        weight_copy((me + i) % 32).wait_send()
        weight_arrival((me + i) % 32).wait_recv()
        return carry

    lax.fori_loop(1, 32, end_weight, 0)


def gather_all(rows, weight):
    count = 32
    return pl.pallas_call(
        gather_kernel,
        out_shape=(
            jax.ShapeDtypeStruct((count,) + rows.shape, rows.dtype),
            jax.ShapeDtypeStruct((count,) + weight.shape, weight.dtype),
        ),
        in_specs=[pl.BlockSpec(memory_space=pltpu.VMEM)] * 2,
        out_specs=(pl.BlockSpec(memory_space=pl.ANY), pl.BlockSpec(memory_space=pl.ANY)),
        scratch_shapes=[
            pltpu.SemaphoreType.DMA((5, 16, 2)),
            pltpu.SemaphoreType.DMA((16, 2)),
            pltpu.SemaphoreType.DMA((16, 2)),
            pltpu.SemaphoreType.DMA((32,)),
            pltpu.SemaphoreType.DMA((32,)),
            pltpu.SemaphoreType.DMA((2,)),
        ],
        compiler_params=pltpu.CompilerParams(collective_id=0, has_side_effects=True),
    )(rows, weight)


def dispatched(out_grad, slot_of, send_gate, capacity):
    experts, tok_count = slot_of.shape
    pick = (slot_of[:, None, :] == jnp.arange(capacity, dtype=jnp.float32)[None, :, None]).astype(jnp.bfloat16)
    rows = jnp.einsum("ect,td->ecd", pick, out_grad, preferred_element_type=jnp.float32).astype(jnp.bfloat16)
    return lax.all_to_all(rows.reshape(experts * capacity, -1), "expert", split_axis=0, concat_axis=0, tiled=True)


def per_device(use_gather, out_grad, inputs, router_weight, routes, saved_hidden, down_weight):
    precise = lax.Precision.HIGHEST
    experts = lax.axis_size("expert")
    tok_count, top_count = routes.shape
    slot_count = saved_hidden.shape[0]
    capacity = slot_count // experts
    model_width = out_grad.shape[1]
    rows_dev = router_weight.shape[0]
    if use_gather:
        all_rows, router_full = gather_all(out_grad, router_weight.reshape(-1, 128))
        router_full = router_full.reshape(model_width, experts)
    else:
        router_full = lax.all_gather(router_weight, "expert", axis=0, tiled=True)
    inputs_wide = inputs.astype(jnp.float32)
    logits = jnp.dot(inputs_wide, router_full, precision=precise)
    scores = jax.nn.sigmoid(logits)
    expert_grid = jnp.arange(experts, dtype=jnp.int32)
    named = routes[:, :, None] == expert_grid[None, None, :]
    hot = jnp.any(named, axis=1)
    chosen = jnp.where(hot, scores, 0.0)
    totals = jnp.sum(chosen, axis=1, keepdims=True)
    gates = ROUTE_SCALE * chosen / totals
    token_grid = jnp.arange(tok_count)
    before = (token_grid[None, :] < token_grid[:, None]).astype(jnp.bfloat16)
    position = jnp.dot(before, hot.astype(jnp.bfloat16), preferred_element_type=jnp.float32)
    position = jnp.where(hot, position, -1.0)
    sent = jnp.stack([position.T, gates.astype(jnp.bfloat16).astype(jnp.float32).T], axis=1)
    got = lax.all_to_all(sent, "expert", split_axis=0, concat_axis=0, tiled=True)
    pick_slot, pick_gate = got[:, 0], got[:, 1]
    pick = pick_slot[:, None, :] == jnp.arange(capacity, dtype=jnp.float32)[None, :, None]
    if use_gather:
        rows = jnp.einsum("sct,std->scd", pick.astype(jnp.bfloat16), all_rows, preferred_element_type=jnp.float32)
        rows = rows.astype(jnp.bfloat16).reshape(slot_count, model_width)
    else:
        rows = dispatched(out_grad, position.T, None, capacity)
    slot_gate = jnp.sum(jnp.where(pick, pick_gate[:, None, :], 0.0), axis=2)
    raw_grad = lax.dot_general(
        rows,
        lax.all_gather(down_weight, "dp", axis=2, tiled=True)[0],
        (((1,), (1,)), ((), ())),
        preferred_element_type=jnp.float32,
    )
    gate_terms = jnp.sum(raw_grad * saved_hidden.astype(jnp.float32), axis=1)
    hidden_grad = (slot_gate.reshape(-1)[:, None] * raw_grad).astype(jnp.bfloat16)
    back = jnp.sum(jnp.where(pick, gate_terms.reshape(experts, capacity)[:, :, None], 0.0), axis=1)
    returned = lax.all_to_all(back, "expert", split_axis=0, concat_axis=0, tiled=True).T
    gate_grad = jnp.sum(jnp.where(named, returned[:, None, :], 0.0), axis=2)
    weighted = jnp.sum(returned * gates, axis=1, keepdims=True)
    logit_grad = jnp.where(hot, (ROUTE_SCALE * returned - weighted) / totals * chosen * (1.0 - chosen), 0.0)
    input_grad = jnp.dot(logit_grad, router_full.T, precision=precise).astype(jnp.bfloat16)
    part = jnp.dot(inputs_wide.T, logit_grad, precision=precise)
    terms = lax.all_to_all(part.reshape(experts, -1, 128), "expert", split_axis=0, concat_axis=0, tiled=True)
    router_grad = lax.psum(jnp.sum(terms, axis=0).reshape(rows_dev, experts), "dp")
    return (hidden_grad, input_grad, gate_grad, router_grad)


def solution(mesh):
    use_gather = mesh.shape["expert"] == 32 and mesh.shape["dp"] == 1

    def run(*args):
        return per_device(use_gather, *args)

    return jax.shard_map(
        run,
        mesh=mesh,
        in_specs=(
            P(("dp", "expert"), None),
            P(("dp", "expert"), None),
            P("expert", None),
            P(("dp", "expert"), None),
            P(("dp", "expert"), None),
            P("expert", None, "dp"),
        ),
        out_specs=(
            P(("dp", "expert"), None),
            P(("dp", "expert"), None),
            P(("dp", "expert"), None),
            P("expert", None),
        ),
        check_vma=False,
    )
```

```python
import jax
import jax.numpy as jnp
from jax import lax
from jax.experimental import pallas as pl
from jax.experimental.pallas import tpu as pltpu
from jax.sharding import PartitionSpec as P

ROUTE_SCALE = 2.5
MESH_ID = pl.DeviceIdType.MESH
UP, DOWN, XWAY, YWAY, PAIR = range(5)


def gather_kernel(rows_ref, weight_ref, place_ref, down_ref, raw_out, weight_out, all_rows, all_places, down, picked, raw,
                  send, recv, pair_recv, weight_send, weight_recv, place_send, place_recv, own_sem, raw_sem):
    me = lax.axis_index("expert")
    core, x, y, z = me % 2, (me // 2) % 2, (me // 4) % 2, me // 8
    tok_count = rows_ref.shape[0]
    half = tok_count // 2
    pair_rows = raw.shape[1] // 4

    def number(xx, yy, zz, cc):
        return ((zz * 2 + yy) * 2 + xx) * 2 + cc

    own_copies = [
        pltpu.make_async_copy(rows_ref, all_rows.at[me // 2, pl.ds(core * tok_count, tok_count)], own_sem.at[0]),
        pltpu.make_async_copy(weight_ref, weight_out.at[me], own_sem.at[1]),
        pltpu.make_async_copy(place_ref.at[me], all_places.at[me], own_sem.at[2]),
        pltpu.make_async_copy(down_ref, down, own_sem.at[3]),
    ]
    for own in own_copies:
        own.start()
    barrier = pltpu.get_barrier_semaphore()

    def greet(i, carry):
        pl.semaphore_signal(barrier, inc=1, device_id={"expert": (me + i) % 32}, device_id_type=MESH_ID)
        return carry

    lax.fori_loop(1, 32, greet, 0)
    own_copies[0].wait()
    pl.semaphore_wait(barrier, 31)

    def weight_copy(to, owner):
        return pltpu.make_async_remote_copy(
            src_ref=weight_ref, dst_ref=weight_out.at[owner], send_sem=weight_send.at[to], recv_sem=weight_recv.at[owner],
            device_id={"expert": to}, device_id_type=MESH_ID)

    def place_copy(to, owner):
        return pltpu.make_async_remote_copy(
            src_ref=place_ref.at[to], dst_ref=all_places.at[owner], send_sem=place_send.at[to], recv_sem=place_recv.at[owner],
            device_id={"expert": to}, device_id_type=MESH_ID)

    def block(origin, part):
        return all_rows.at[origin // 2, pl.ds((origin % 2) * tok_count + part * half, half)]

    def copy(origin, part, way):
        target = {
            UP: lambda: number(x, y, z + 1, core), DOWN: lambda: number(x, y, z - 1, core),
            XWAY: lambda: number(1 - x, y, z, core), YWAY: lambda: number(x, 1 - y, z, core),
            PAIR: lambda: number(x, y, z, 1 - core)}[way]()
        chip = origin // 2
        arrived = pair_recv if way == PAIR else recv
        return pltpu.make_async_remote_copy(
            src_ref=block(origin, part), dst_ref=block(origin, part),
            send_sem=send.at[way, chip, part], recv_sem=arrived.at[chip, part],
            device_id={"expert": target}, device_id_type=MESH_ID)

    def plane(j):
        inner = jnp.where(j == 3, 3, (j + 1) % 3)
        return jnp.where(z == 0, j, jnp.where(z == 3, 3 - j, jnp.where(z == 1, inner, 3 - inner)))

    def along_z(j):
        zz = plane(j)
        origin = number(x, y, zz, core)
        for part in range(2):
            pl.when(j > 0)(lambda: copy(origin, part, XWAY).wait_recv())
            pl.when((zz >= z) & (z >= 1))(lambda: copy(origin, part, DOWN).start())
            pl.when((zz <= z) & (z <= 2))(lambda: copy(origin, part, UP).start())
            copy(origin, part, XWAY).start()
            copy(origin, part, YWAY).start()
            copy(origin, part, PAIR).start()

    def across(j):
        zz = plane(j)
        from_x, from_y = number(1 - x, y, zz, core), number(x, 1 - y, zz, core)
        for part in range(2):
            copy(from_x, part, XWAY).wait_recv()
            if part == 0:
                copy(from_x, part, YWAY).start()
            copy(from_x, part, PAIR).start()
            copy(from_y, part, YWAY).wait_recv()
            if part == 1:
                copy(from_y, part, XWAY).start()
            copy(from_y, part, PAIR).start()

    def diagonal(j):
        origin = number(1 - x, 1 - y, plane(j), core)
        for part in range(2):
            copy(origin, part, XWAY).wait_recv()
            copy(origin, part, PAIR).start()

    def finish(j):
        zz = plane(j)
        origin = number(x, y, zz, core)
        for part in range(2):
            pl.when((zz >= z) & (z >= 1))(lambda: copy(origin, part, DOWN).wait_send())
            pl.when((zz <= z) & (z <= 2))(lambda: copy(origin, part, UP).wait_send())
            copy(origin, part, XWAY).wait_send()
            copy(origin, part, YWAY).wait_send()
        copy(number(1 - x, y, zz, core), 0, YWAY).wait_send()
        copy(number(x, 1 - y, zz, core), 1, XWAY).wait_send()

    def raw_copy(zz):
        return pltpu.make_async_copy(raw.at[zz], raw_out.at[zz], raw_sem.at[zz])

    def compute(j):
        zz = plane(j)
        for i in range(4):
            chip = zz * 4 + i
            for part in range(2):
                copy(chip * 2 + 1 - core, part, PAIR).wait_recv()
            places = jnp.concatenate([all_places[chip * 2], all_places[chip * 2 + 1]], axis=1)
            slots = lax.broadcasted_iota(jnp.int32, (pair_rows, 2 * tok_count), 0).astype(jnp.float32)
            pick = jnp.where(places == slots, 1.0, 0.0).astype(jnp.bfloat16)

            @pl.loop(0, all_rows.shape[2] // 512)
            def _(n):
                columns = pl.ds(pl.multiple_of(n * 512, 512), 512)
                found = jnp.dot(pick, all_rows[chip, :, columns], preferred_element_type=jnp.float32)
                picked[pl.ds(i * pair_rows, pair_rows), columns] = found.astype(jnp.bfloat16)

        @pl.loop(0, down.shape[0] // 256)
        def _(n):
            units = pl.ds(pl.multiple_of(n * 256, 256), 256)
            raw[zz, :, units] = lax.dot_general(
                picked[...], down[units, :], (((1,), (1,)), ((), ())), preferred_element_type=jnp.float32)

        raw_copy(zz).start()

    def send_small(i, carry):
        to = (me + i) % 32
        place_copy(to, me).start()
        weight_copy(to, me).start()
        return carry

    def end_small(i, carry):
        other = (me + i) % 32
        place_copy(other, me).wait_send()
        place_copy(other, other).wait_recv()
        weight_copy(other, me).wait_send()
        weight_copy(other, other).wait_recv()
        return carry

    along_z(0)
    lax.fori_loop(1, 32, send_small, 0)
    for own in own_copies[1:]:
        own.wait()

    def step(j, carry):
        pl.when(j < 4)(lambda: along_z(j))
        pl.when(j < 5)(lambda: across(j - 1))

        @pl.when(j == 2)
        def _():
            lax.fori_loop(1, 32, end_small, 0)

        @pl.when(j >= 2)
        def _():
            diagonal(j - 2)
            compute(j - 2)

        return carry

    lax.fori_loop(1, 6, step, 0)

    def end(j, carry):
        finish(j)
        raw_copy(j).wait()
        return carry

    lax.fori_loop(0, 4, end, 0)

    def end_pair(i, carry):
        for part in range(2):
            copy(i * 2 + core, part, PAIR).wait_send()
        return carry

    lax.fori_loop(0, 16, end_pair, 0)


def gather_all(rows, weight, places, down, slot_count):
    tok_count, model_width = rows.shape
    hidden = down.shape[0]
    return pl.pallas_call(
        gather_kernel,
        out_shape=(
            jax.ShapeDtypeStruct((4, slot_count // 4, hidden), jnp.float32),
            jax.ShapeDtypeStruct((32,) + weight.shape, weight.dtype),
        ),
        in_specs=[pl.BlockSpec(memory_space=pltpu.VMEM)] * 3 + [pl.BlockSpec(memory_space=pl.ANY)],
        out_specs=(pl.BlockSpec(memory_space=pl.ANY), pl.BlockSpec(memory_space=pl.ANY)),
        scratch_shapes=[
            pltpu.VMEM((16, 2 * tok_count, model_width), jnp.bfloat16),
            pltpu.VMEM((32, 1, tok_count), jnp.float32),
            pltpu.VMEM(down.shape, jnp.bfloat16),
            pltpu.VMEM((slot_count // 4, model_width), jnp.bfloat16),
            pltpu.VMEM((4, slot_count // 4, hidden), jnp.float32),
            pltpu.SemaphoreType.DMA((5, 16, 2)),
            pltpu.SemaphoreType.DMA((16, 2)),
            pltpu.SemaphoreType.DMA((16, 2)),
            pltpu.SemaphoreType.DMA((32,)),
            pltpu.SemaphoreType.DMA((32,)),
            pltpu.SemaphoreType.DMA((32,)),
            pltpu.SemaphoreType.DMA((32,)),
            pltpu.SemaphoreType.DMA((4,)),
            pltpu.SemaphoreType.DMA((4,)),
        ],
        compiler_params=pltpu.CompilerParams(collective_id=0, has_side_effects=True, vmem_limit_bytes=60000 * 1024),
    )(rows, weight, places, down)


def dispatched(out_grad, position, capacity, experts):
    pick = (position.T[:, None, :] == jnp.arange(capacity, dtype=jnp.float32)[None, :, None]).astype(jnp.bfloat16)
    rows = jnp.einsum("ect,td->ecd", pick, out_grad, preferred_element_type=jnp.float32).astype(jnp.bfloat16)
    return lax.all_to_all(rows.reshape(experts * capacity, -1), "expert", split_axis=0, concat_axis=0, tiled=True)


def per_device(use_gather, out_grad, inputs, router_weight, routes, saved_hidden, down_weight):
    precise = lax.Precision.HIGHEST
    experts = lax.axis_size("expert")
    tok_count = routes.shape[0]
    slot_count = saved_hidden.shape[0]
    capacity = slot_count // experts
    model_width = out_grad.shape[1]
    rows_dev = router_weight.shape[0]
    expert_grid = jnp.arange(experts, dtype=jnp.int32)
    named = routes[:, :, None] == expert_grid[None, None, :]
    hot = jnp.any(named, axis=1)
    token_grid = jnp.arange(tok_count)
    before = (token_grid[None, :] < token_grid[:, None]).astype(jnp.bfloat16)
    position = jnp.dot(before, hot.astype(jnp.bfloat16), preferred_element_type=jnp.float32)
    position = jnp.where(hot, position, -1.0)
    if use_gather:
        shift = (lax.axis_index("expert") % 2 * capacity).astype(jnp.float32)
        places = jnp.where(hot, position + shift, -1.0).T[:, None, :]
        raw_grad, router_full = gather_all(out_grad, router_weight.reshape(-1, 128), places, down_weight[0], slot_count)
        raw_grad = raw_grad.reshape(slot_count, -1)
        router_full = router_full.reshape(model_width, experts)
    else:
        router_full = lax.all_gather(router_weight, "expert", axis=0, tiled=True)
        raw_grad = lax.dot_general(
            dispatched(out_grad, position, capacity, experts),
            lax.all_gather(down_weight, "dp", axis=2, tiled=True)[0],
            (((1,), (1,)), ((), ())),
            preferred_element_type=jnp.float32,
        )
    inputs_wide = inputs.astype(jnp.float32)
    logits = jnp.dot(inputs_wide, router_full, precision=precise)
    scores = jax.nn.sigmoid(logits)
    chosen = jnp.where(hot, scores, 0.0)
    totals = jnp.sum(chosen, axis=1, keepdims=True)
    gates = ROUTE_SCALE * chosen / totals
    sent = jnp.stack([position.T, lax.reduce_precision(gates, 8, 7).T], axis=1)
    got = lax.all_to_all(sent, "expert", split_axis=0, concat_axis=0, tiled=True)
    pick_slot, pick_gate = got[:, 0], got[:, 1]
    pick = pick_slot[:, None, :] == jnp.arange(capacity, dtype=jnp.float32)[None, :, None]
    slot_gate = jnp.sum(jnp.where(pick, pick_gate[:, None, :], 0.0), axis=2)
    gate_terms = jnp.sum(raw_grad * saved_hidden.astype(jnp.float32), axis=1)
    hidden_grad = (slot_gate.reshape(-1)[:, None] * raw_grad).astype(jnp.bfloat16)
    back = jnp.sum(jnp.where(pick, gate_terms.reshape(experts, capacity)[:, :, None], 0.0), axis=1)
    returned = lax.all_to_all(back, "expert", split_axis=0, concat_axis=0, tiled=True).T
    gate_grad = jnp.sum(jnp.where(named, returned[:, None, :], 0.0), axis=2)
    weighted = jnp.sum(returned * gates, axis=1, keepdims=True)
    logit_grad = jnp.where(hot, (ROUTE_SCALE * returned - weighted) / totals * chosen * (1.0 - chosen), 0.0)
    input_grad = jnp.dot(logit_grad, router_full.T, precision=precise).astype(jnp.bfloat16)
    part = jnp.dot(inputs_wide.T, logit_grad, precision=precise)
    terms = lax.all_to_all(part.reshape(experts, -1, 128), "expert", split_axis=0, concat_axis=0, tiled=True)
    router_grad = lax.psum(jnp.sum(terms, axis=0).reshape(rows_dev, experts), "dp")
    return (hidden_grad, input_grad, gate_grad, router_grad)


def solution(mesh):
    use_gather = mesh.shape["expert"] == 32 and mesh.shape["dp"] == 1

    def run(*args):
        return per_device(use_gather, *args)

    return jax.shard_map(
        run,
        mesh=mesh,
        in_specs=(
            P(("dp", "expert"), None),
            P(("dp", "expert"), None),
            P("expert", None),
            P(("dp", "expert"), None),
            P(("dp", "expert"), None),
            P("expert", None, "dp"),
        ),
        out_specs=(
            P(("dp", "expert"), None),
            P(("dp", "expert"), None),
            P(("dp", "expert"), None),
            P("expert", None),
        ),
        check_vma=False,
    )
```

```python
import jax
import jax.numpy as jnp
from jax import lax
from jax.experimental import pallas as pl
from jax.experimental.pallas import tpu as pltpu
from jax.sharding import PartitionSpec as P

ROUTE_SCALE = 2.5
MESH_ID = pl.DeviceIdType.MESH
UP, DOWN, XWAY, YWAY, PAIR = range(5)


def gather_kernel(rows_ref, weight_ref, place_ref, down_ref, raw_out, weight_out, all_rows, all_places, down, picked, raw,
                  send, recv, pair_recv, weight_send, weight_recv, place_send, place_recv, own_sem, raw_sem):
    me = lax.axis_index("expert")
    core, x, y, z = me % 2, (me // 2) % 2, (me // 4) % 2, me // 8
    tok_count = rows_ref.shape[0]
    most = tok_count * 3 // 8
    starts, sizes = (0, most, 2 * most), (most, most, tok_count - 2 * most)
    pair_rows = raw.shape[1] // 4

    def number(xx, yy, zz, cc):
        return ((zz * 2 + yy) * 2 + xx) * 2 + cc

    own_copies = [
        pltpu.make_async_copy(rows_ref, all_rows.at[me // 2, pl.ds(core * tok_count, tok_count)], own_sem.at[0]),
        pltpu.make_async_copy(weight_ref, weight_out.at[me], own_sem.at[1]),
        pltpu.make_async_copy(place_ref.at[me], all_places.at[me], own_sem.at[2]),
        pltpu.make_async_copy(down_ref, down, own_sem.at[3]),
    ]
    for own in own_copies:
        own.start()
    barrier = pltpu.get_barrier_semaphore()

    def greet(i, carry):
        pl.semaphore_signal(barrier, inc=1, device_id={"expert": (me + i) % 32}, device_id_type=MESH_ID)
        return carry

    lax.fori_loop(1, 32, greet, 0)
    own_copies[0].wait()
    pl.semaphore_wait(barrier, 31)

    def weight_copy(to, owner):
        return pltpu.make_async_remote_copy(
            src_ref=weight_ref, dst_ref=weight_out.at[owner], send_sem=weight_send.at[to], recv_sem=weight_recv.at[owner],
            device_id={"expert": to}, device_id_type=MESH_ID)

    def place_copy(to, owner):
        return pltpu.make_async_remote_copy(
            src_ref=place_ref.at[to], dst_ref=all_places.at[owner], send_sem=place_send.at[to], recv_sem=place_recv.at[owner],
            device_id={"expert": to}, device_id_type=MESH_ID)

    def block(origin, part):
        return all_rows.at[origin // 2, pl.ds((origin % 2) * tok_count + starts[part], sizes[part])]

    def copy(origin, part, way):
        target = {
            UP: lambda: number(x, y, z + 1, core), DOWN: lambda: number(x, y, z - 1, core),
            XWAY: lambda: number(1 - x, y, z, core), YWAY: lambda: number(x, 1 - y, z, core),
            PAIR: lambda: number(x, y, z, 1 - core)}[way]()
        chip = origin // 2
        arrived = pair_recv if way == PAIR else recv
        return pltpu.make_async_remote_copy(
            src_ref=block(origin, part), dst_ref=block(origin, part),
            send_sem=send.at[way, chip, part], recv_sem=arrived.at[chip, part],
            device_id={"expert": target}, device_id_type=MESH_ID)

    def plane(j):
        inner = jnp.where(j == 3, 3, (j + 1) % 3)
        return jnp.where(z == 0, j, jnp.where(z == 3, 3 - j, jnp.where(z == 1, inner, 3 - inner)))

    def vertical(origin, zz, part, act):
        pl.when((zz >= z) & (z >= 1))(lambda: act(copy(origin, part, DOWN)))
        pl.when((zz <= z) & (z <= 2))(lambda: act(copy(origin, part, UP)))

    def start(item):
        item.start()

    def wait_send(item):
        item.wait_send()

    def along_z(j):
        zz = plane(j)
        origin = number(x, y, zz, core)
        for part in range(2):
            pl.when(j > 0)(lambda: copy(origin, part, XWAY).wait_recv())
            pl.when((zz >= z) & (z >= 1))(lambda: copy(origin, part, DOWN).start())
            pl.when((zz <= z) & (z <= 2))(lambda: copy(origin, part, UP).start())
            copy(origin, part, XWAY).start()
            copy(origin, part, YWAY).start()
            copy(origin, part, PAIR).start()

        @pl.when(j == 0)
        def _():
            copy(origin, 2, XWAY).start()
            copy(origin, 2, YWAY).start()
            vertical(origin, zz, 2, start)
            copy(origin, 2, PAIR).start()

    def spread(j):
        zz = plane(j)
        for i in range(4):
            origin = (zz * 4 + i) * 2 + core
            copy(origin, 2, UP).wait_recv()
            vertical(origin, zz, 2, start)
            copy(origin, 2, PAIR).start()

    def across(j):
        zz = plane(j)
        from_x, from_y = number(1 - x, y, zz, core), number(x, 1 - y, zz, core)
        for part in range(2):
            copy(from_x, part, XWAY).wait_recv()
            if part == 0:
                copy(from_x, part, YWAY).start()
            copy(from_x, part, PAIR).start()
            copy(from_y, part, YWAY).wait_recv()
            if part == 1:
                copy(from_y, part, XWAY).start()
            copy(from_y, part, PAIR).start()

        @pl.when(j == 0)
        def _():
            copy(from_x, 2, XWAY).wait_recv()
            pl.when(core == 0)(lambda: copy(from_x, 2, YWAY).start())
            vertical(from_x, zz, 2, start)
            copy(from_x, 2, PAIR).start()
            copy(from_y, 2, YWAY).wait_recv()
            pl.when(core == 1)(lambda: copy(from_y, 2, XWAY).start())
            vertical(from_y, zz, 2, start)
            copy(from_y, 2, PAIR).start()

    def diagonal(j):
        origin = number(1 - x, 1 - y, plane(j), core)
        for part in range(2):
            copy(origin, part, XWAY).wait_recv()
            copy(origin, part, PAIR).start()

        @pl.when(j == 0)
        def _():
            copy(origin, 2, XWAY).wait_recv()
            vertical(origin, z, 2, start)
            copy(origin, 2, PAIR).start()

    def finish(j):
        zz = plane(j)
        origin = number(x, y, zz, core)
        for part in range(2):
            pl.when((zz >= z) & (z >= 1))(lambda: copy(origin, part, DOWN).wait_send())
            pl.when((zz <= z) & (z <= 2))(lambda: copy(origin, part, UP).wait_send())
            copy(origin, part, XWAY).wait_send()
            copy(origin, part, YWAY).wait_send()
        copy(number(1 - x, y, zz, core), 0, YWAY).wait_send()
        copy(number(x, 1 - y, zz, core), 1, XWAY).wait_send()
        for i in range(4):
            vertical((zz * 4 + i) * 2 + core, zz, 2, wait_send)

        @pl.when(j == 0)
        def _():
            copy(origin, 2, XWAY).wait_send()
            copy(origin, 2, YWAY).wait_send()
            pl.when(core == 0)(lambda: copy(number(1 - x, y, z, core), 2, YWAY).wait_send())
            pl.when(core == 1)(lambda: copy(number(x, 1 - y, z, core), 2, XWAY).wait_send())

    def raw_copy(zz):
        return pltpu.make_async_copy(raw.at[zz], raw_out.at[zz], raw_sem.at[zz])

    def compute(j):
        zz = plane(j)
        for i in range(4):
            chip = zz * 4 + i
            for part in range(3):
                copy(chip * 2 + 1 - core, part, PAIR).wait_recv()
            places = jnp.concatenate([all_places[chip * 2], all_places[chip * 2 + 1]], axis=1)
            slots = lax.broadcasted_iota(jnp.int32, (pair_rows, 2 * tok_count), 0).astype(jnp.float32)
            pick = jnp.where(places == slots, 1.0, 0.0).astype(jnp.bfloat16)

            @pl.loop(0, all_rows.shape[2] // 512)
            def _(n):
                columns = pl.ds(pl.multiple_of(n * 512, 512), 512)
                found = jnp.dot(pick, all_rows[chip, :, columns], preferred_element_type=jnp.float32)
                picked[pl.ds(i * pair_rows, pair_rows), columns] = found.astype(jnp.bfloat16)

        @pl.loop(0, down.shape[0] // 256)
        def _(n):
            units = pl.ds(pl.multiple_of(n * 256, 256), 256)
            raw[zz, :, units] = lax.dot_general(
                picked[...], down[units, :], (((1,), (1,)), ((), ())), preferred_element_type=jnp.float32)

        raw_copy(zz).start()

    def send_small(i, carry):
        to = (me + i) % 32
        place_copy(to, me).start()
        weight_copy(to, me).start()
        return carry

    def end_small(i, carry):
        other = (me + i) % 32
        place_copy(other, me).wait_send()
        place_copy(other, other).wait_recv()
        weight_copy(other, me).wait_send()
        weight_copy(other, other).wait_recv()
        return carry

    along_z(0)
    lax.fori_loop(1, 32, send_small, 0)
    for own in own_copies[1:]:
        own.wait()

    def step(j, carry):
        pl.when(j < 4)(lambda: along_z(j))
        pl.when(j < 5)(lambda: across(j - 1))

        @pl.when(j == 2)
        def _():
            lax.fori_loop(1, 32, end_small, 0)

        @pl.when(j >= 2)
        def _():
            diagonal(j - 2)
            pl.when(j <= 4)(lambda: spread(j - 1))
            compute(j - 2)

        return carry

    lax.fori_loop(1, 6, step, 0)

    def end(j, carry):
        finish(j)
        raw_copy(j).wait()
        return carry

    lax.fori_loop(0, 4, end, 0)

    def end_pair(i, carry):
        for part in range(3):
            copy(i * 2 + core, part, PAIR).wait_send()
        return carry

    lax.fori_loop(0, 16, end_pair, 0)


def gather_all(rows, weight, places, down, slot_count):
    tok_count, model_width = rows.shape
    hidden = down.shape[0]
    return pl.pallas_call(
        gather_kernel,
        out_shape=(
            jax.ShapeDtypeStruct((4, slot_count // 4, hidden), jnp.float32),
            jax.ShapeDtypeStruct((32,) + weight.shape, weight.dtype),
        ),
        in_specs=[pl.BlockSpec(memory_space=pltpu.VMEM)] * 3 + [pl.BlockSpec(memory_space=pl.ANY)],
        out_specs=(pl.BlockSpec(memory_space=pl.ANY), pl.BlockSpec(memory_space=pl.ANY)),
        scratch_shapes=[
            pltpu.VMEM((16, 2 * tok_count, model_width), jnp.bfloat16),
            pltpu.VMEM((32, 1, tok_count), jnp.float32),
            pltpu.VMEM(down.shape, jnp.bfloat16),
            pltpu.VMEM((slot_count // 4, model_width), jnp.bfloat16),
            pltpu.VMEM((4, slot_count // 4, hidden), jnp.float32),
            pltpu.SemaphoreType.DMA((5, 16, 3)),
            pltpu.SemaphoreType.DMA((16, 3)),
            pltpu.SemaphoreType.DMA((16, 3)),
            pltpu.SemaphoreType.DMA((32,)),
            pltpu.SemaphoreType.DMA((32,)),
            pltpu.SemaphoreType.DMA((32,)),
            pltpu.SemaphoreType.DMA((32,)),
            pltpu.SemaphoreType.DMA((4,)),
            pltpu.SemaphoreType.DMA((4,)),
        ],
        compiler_params=pltpu.CompilerParams(collective_id=0, has_side_effects=True, vmem_limit_bytes=60000 * 1024),
    )(rows, weight, places, down)


def dispatched(out_grad, position, capacity, experts):
    pick = (position.T[:, None, :] == jnp.arange(capacity, dtype=jnp.float32)[None, :, None]).astype(jnp.bfloat16)
    rows = jnp.einsum("ect,td->ecd", pick, out_grad, preferred_element_type=jnp.float32).astype(jnp.bfloat16)
    return lax.all_to_all(rows.reshape(experts * capacity, -1), "expert", split_axis=0, concat_axis=0, tiled=True)


def per_device(use_gather, out_grad, inputs, router_weight, routes, saved_hidden, down_weight):
    precise = lax.Precision.HIGHEST
    experts = lax.axis_size("expert")
    tok_count = routes.shape[0]
    slot_count = saved_hidden.shape[0]
    capacity = slot_count // experts
    model_width = out_grad.shape[1]
    rows_dev = router_weight.shape[0]
    expert_grid = jnp.arange(experts, dtype=jnp.int32)
    named = routes[:, :, None] == expert_grid[None, None, :]
    hot = jnp.any(named, axis=1)
    token_grid = jnp.arange(tok_count)
    before = (token_grid[None, :] < token_grid[:, None]).astype(jnp.bfloat16)
    position = jnp.dot(before, hot.astype(jnp.bfloat16), preferred_element_type=jnp.float32)
    position = jnp.where(hot, position, -1.0)
    if use_gather:
        shift = (lax.axis_index("expert") % 2 * capacity).astype(jnp.float32)
        places = jnp.where(hot, position + shift, -1.0).T[:, None, :]
        raw_grad, router_full = gather_all(out_grad, router_weight.reshape(-1, 128), places, down_weight[0], slot_count)
        raw_grad = raw_grad.reshape(slot_count, -1)
        router_full = router_full.reshape(model_width, experts)
    else:
        router_full = lax.all_gather(router_weight, "expert", axis=0, tiled=True)
        raw_grad = lax.dot_general(
            dispatched(out_grad, position, capacity, experts),
            lax.all_gather(down_weight, "dp", axis=2, tiled=True)[0],
            (((1,), (1,)), ((), ())),
            preferred_element_type=jnp.float32,
        )
    inputs_wide = inputs.astype(jnp.float32)
    logits = jnp.dot(inputs_wide, router_full, precision=precise)
    scores = jax.nn.sigmoid(logits)
    chosen = jnp.where(hot, scores, 0.0)
    totals = jnp.sum(chosen, axis=1, keepdims=True)
    gates = ROUTE_SCALE * chosen / totals
    sent = jnp.stack([position.T, lax.reduce_precision(gates, 8, 7).T], axis=1)
    got = lax.all_to_all(sent, "expert", split_axis=0, concat_axis=0, tiled=True)
    pick_slot, pick_gate = got[:, 0], got[:, 1]
    pick = pick_slot[:, None, :] == jnp.arange(capacity, dtype=jnp.float32)[None, :, None]
    slot_gate = jnp.sum(jnp.where(pick, pick_gate[:, None, :], 0.0), axis=2)
    gate_terms = jnp.sum(raw_grad * saved_hidden.astype(jnp.float32), axis=1)
    hidden_grad = (slot_gate.reshape(-1)[:, None] * raw_grad).astype(jnp.bfloat16)
    back = jnp.sum(jnp.where(pick, gate_terms.reshape(experts, capacity)[:, :, None], 0.0), axis=1)
    returned = lax.all_to_all(back, "expert", split_axis=0, concat_axis=0, tiled=True).T
    gate_grad = jnp.sum(jnp.where(named, returned[:, None, :], 0.0), axis=2)
    weighted = jnp.sum(returned * gates, axis=1, keepdims=True)
    logit_grad = jnp.where(hot, (ROUTE_SCALE * returned - weighted) / totals * chosen * (1.0 - chosen), 0.0)
    input_grad = jnp.dot(logit_grad, router_full.T, precision=precise).astype(jnp.bfloat16)
    part = jnp.dot(inputs_wide.T, logit_grad, precision=precise)
    terms = lax.all_to_all(part.reshape(experts, -1, 128), "expert", split_axis=0, concat_axis=0, tiled=True)
    router_grad = lax.psum(jnp.sum(terms, axis=0).reshape(rows_dev, experts), "dp")
    return (hidden_grad, input_grad, gate_grad, router_grad)


def solution(mesh):
    use_gather = mesh.shape["expert"] == 32 and mesh.shape["dp"] == 1

    def run(*args):
        return per_device(use_gather, *args)

    return jax.shard_map(
        run,
        mesh=mesh,
        in_specs=(
            P(("dp", "expert"), None),
            P(("dp", "expert"), None),
            P("expert", None),
            P(("dp", "expert"), None),
            P(("dp", "expert"), None),
            P("expert", None, "dp"),
        ),
        out_specs=(
            P(("dp", "expert"), None),
            P(("dp", "expert"), None),
            P(("dp", "expert"), None),
            P("expert", None),
        ),
        check_vma=False,
    )
```
